32 devices in a mesh: req: 8 (over z, y), tp: 4 (over x, core).
Axes of the slice: x: 2, y: 2, z: 4, core: 2. Of those that a mesh axis runs over, the one named last changes fastest.
Arguments:
- hidden_in: bfloat16 [512, 2048], P('req'), may hold values from -6 to 6
- queries: bfloat16 [512, 2048], P('req', 'tp'), may hold values from -200 to 200, as said below
- keys_new: bfloat16 [512, 2048], P('req', 'tp'), may hold values from -6 to 6
- values_new: bfloat16 [512, 2048], P('req', 'tp'), may hold values from -6 to 6
- prefix_keys: bfloat16 [8, 16, 2048], P('req', None, 'tp'), may hold values from -6 to 6
- prefix_values: bfloat16 [8, 16, 2048], P('req', None, 'tp'), may hold values from -6 to 6
- block_group: int32 [8], P('req'), may hold values from 0 to 1, as said below
- req_group: int32 [8], P('req'), may hold values from 0 to 1
- lengths: int32 [8], P('req'), may hold values from 1 to 64, 320 in all
- w_out: bfloat16 [2048, 2048], P('tp'), may hold values from -0.125 to 0.125
- norm_gain: bfloat16 [2048], replicated, may hold values from 0.25 to 1.75
- w_router: float32 [2048, 64], replicated, may hold values from -7 to 7
- routes: int32 [512, 8], P('req'), may hold values from 0 to 63, all different within a row; in each aligned block of 64 rows (0 to 63, 64 to 127, ...) at most 10 rows name the same one
- w_gate: bfloat16 [128, 2048, 512], P('req', None, 'tp'), may hold values from -0.125 to 0.125
- w_up: bfloat16 [128, 2048, 512], P('req', None, 'tp'), may hold values from -0.125 to 0.125
- w_down: bfloat16 [128, 512, 2048], P('req', 'tp'), may hold values from -0.1875 to 0.1875
Outputs:
- layer_out: bfloat16 [512, 2048], P('req', 'tp')
The draws below stay inside these ranges and needn't reach their ends.
Inputs may be any that keep to these rules, and one draw needn't show every extreme that they name: queries: the printed draw and the hidden one differ in row scales. `block_group`: exactly half of the 8 cache blocks belong to each group. `routes`: within the rows of one request, each expert is named by at most 10 rows, a bound that some block reaches. `lengths`: each request has at least one live suffix slot, and some request has all 64.
All inputs are finite; a program needn't handle non-finite values. No bound on the sum of `lengths` on one device may be relied on, other than what follows from the above.
Results may differ from the reference program's by a relative error of at most 0.025.
Values may be sent and summed in bfloat16 or wider, within the bound.
A program may use at most 128 MiB of HBM per device.

```python
import math
import jax
import jax.numpy as jnp
import numpy as np
from jax import lax

D = 2048
HEADS = 16
HD = 128
E = 64
FF = 1024
TOPK = 8
TOK_DEV = 64
BLK = 16
REQS = 8
PBLOCKS = 8
TOKENS = 512
CAP = 10
N_TP = 4


def draw_queries(key, part):
    base = jnp.clip(jax.random.normal(jax.random.fold_in(key, 11), (TOKENS, HEADS * HD), jnp.float32), -5.0, 5.0)
    return base.astype(jnp.bfloat16)


def draw_block_group(key, part):
    order = jax.random.permutation(jax.random.fold_in(key, 21), PBLOCKS)
    return (order >= PBLOCKS // 2).astype(jnp.int32)


def draw_w_router(key, part):
    base = jnp.clip(jax.random.normal(jax.random.fold_in(key, 31), (D, E), jnp.float32), -5.0, 5.0) / jnp.sqrt(jnp.float32(D))
    return base


def with_ends(array, stream_key, smallest, high):
    longest = array.shape.index(max(array.shape))
    spots = []
    for shift in (0, 1):
        where = [jax.random.randint(jax.random.fold_in(stream_key, axis), (), 0, length) for axis, length in enumerate(array.shape)]
        where[longest] = (where[longest] + shift) % array.shape[longest]
        spots.append(tuple(where))
    return array.at[spots[0]].set(smallest).at[spots[1]].set(high)


def level_of(stream_key, shape, split, low, largest):
    factor_of, own = 1.0, jax.random.fold_in(stream_key, 6)
    for axis_at, shards_of in split:
        steps = jnp.exp(jax.random.uniform(jax.random.fold_in(own, axis_at), (shards_of,), jnp.float32, low / len(split), largest / len(split)))
        factor_of = factor_of * jnp.repeat(steps, shape[axis_at] // shards_of).reshape([-1 if axis == axis_at else 1 for axis in range(len(shape))])
    return factor_of


def split_up(count, total, bound, lean):
    portions = [(1 << 20) // math.isqrt(rank ** lean) + 1 for rank in range(2, count + 1)]
    surplus, given = total - bound - (count - 1), [1] * (count - 1)
    while surplus > 0:
        movable = [i for i in range(count - 1) if given[i] < bound]
        pool, left = sum([portions[i] for i in movable]), surplus
        for i in movable:
            more = min(bound - given[i], max(1, left * portions[i] // pool), surplus)
            given[i] = given[i] + more
            surplus = surplus - more
    return np.array([bound] + given)


def ragged_sizes(rng, amount, total, reach, slope):
    if amount == 2:
        one = jax.random.randint(rng, (), max(1, total - reach), min(reach, total - 1) + 1)
        return jnp.stack([one, total - one])
    tallies = jnp.asarray(split_up(amount, total, reach, slope), jnp.int32)
    pairs = (amount - 1) // 2
    donor, receiver = tallies[1:1 + 2 * pairs:2], tallies[2:2 + 2 * pairs:2]
    slack = jnp.minimum(donor - 1, reach - receiver)
    moved = jax.random.randint(jax.random.fold_in(rng, 1), (pairs,), 0, 1 << 20) % (slack + 1)
    tallies = tallies.at[1:1 + 2 * pairs:2].set(donor - moved).at[2:2 + 2 * pairs:2].set(receiver + moved)
    return tallies[jax.random.permutation(jax.random.fold_in(rng, 2), amount)]


def shared_out(rng, own, number, rows, number_of, top, bound, slope):
    sequence = jax.random.permutation(rng, number_of)
    heavy_load, common = load_shares(number_of, rows * top, bound, slope, True), load_shares(number_of, rows * top, bound, slope, False)
    places = jnp.arange(number_of)

    def named(sizes, turn):
        used = int((sizes > 0).sum())
        fixed = max(1, used // 4)
        shifted = fixed + (places - fixed + turn * (used - fixed)) % max(1, number_of - fixed)
        return jnp.zeros((number_of,), jnp.int32).at[sequence[jnp.where(places < fixed, places, shifted)]].set(jnp.asarray(sizes, jnp.int32))

    sizes = jnp.where(number % 4 == 0, named(heavy_load, number // 4), named(common, number - number // 4 - 1))
    mixed = jax.random.permutation(jax.random.fold_in(own, 3), number_of)
    source_of, receiver = mixed[0:number_of // 2 * 2:2], mixed[1:number_of // 2 * 2:2]
    slack = jnp.minimum(sizes[source_of] - 1, bound - sizes[receiver]) // 2
    slack = jnp.where((source_of == sequence[0]) | (receiver == sequence[0]) | (sizes[receiver] == 0), 0, jnp.maximum(slack, 0))
    shifted = jax.random.randint(jax.random.fold_in(own, 4), (number_of // 2,), 0, 1 << 20) % (slack + 1)
    sizes = sizes.at[source_of].add(-shifted).at[receiver].add(shifted)
    items = jnp.searchsorted(jnp.cumsum(sizes), jnp.arange(rows * top), side="right").astype(jnp.int32)
    grid = items.reshape(top, rows).T
    grid = grid[jax.random.permutation(jax.random.fold_in(own, 1), rows)]
    turn = jax.random.randint(jax.random.fold_in(own, 2), (rows, 1), 0, top)
    return jnp.take_along_axis(grid, (jnp.arange(top)[None, :] + turn) % top, axis=1)


def load_shares(amount, total, limit, lean, full):
    weights = [(1 << 20) // math.isqrt(rank ** lean) + 1 for rank in range(1, amount + 1)]
    largest = limit if full else min(limit, max(-(-total // amount), total * weights[0] // sum(weights)))
    least = 1 if total - largest >= amount - 1 else 0
    given, spare = [largest] + [least] * (amount - 1), total - largest - least * (amount - 1)
    while spare > 0:
        movable = [i for i in range(1, amount) if given[i] < largest] or [i for i in range(1, amount) if given[i] < limit]
        mass, left = sum([weights[i] for i in movable]), spare
        for i in movable:
            more = min(limit - given[i], max(1, left * weights[i] // mass), spare)
            given[i] = given[i] + more
            spare = spare - more
    return np.array(given)


def gaussian(rng, extent, deviation, bound, split=(), kind=jnp.bfloat16):
    level = level_of(rng, extent, split, -0.22, 0.18) if split else 1.0
    entries = jax.random.normal(rng, extent, jnp.float32) * deviation * level
    return jnp.minimum(jnp.maximum(entries, -bound), bound).astype(kind)


def setup_inputs(seed: int = 0) -> dict:
    key_of = jax.random.split(jax.random.key(seed), 17)
    hidden_in = gaussian(key_of[0], (TOKENS, D), 1.0, 6.0, ((0, 8),))
    queries = draw_queries(jax.random.fold_in(key_of[16], 71), 0)
    keys_new = gaussian(key_of[2], (TOKENS, HEADS * HD), 1.0, 6.0, ((0, 8), (1, 4)))
    values_new = gaussian(key_of[3], (TOKENS, HEADS * HD), 1.0, 6.0, ((0, 8), (1, 4)))
    prefix_keys = gaussian(key_of[4], (PBLOCKS, BLK, HEADS * HD), 1.0, 6.0, ((0, 8), (2, 4)))
    prefix_values = gaussian(key_of[5], (PBLOCKS, BLK, HEADS * HD), 1.0, 6.0, ((0, 8), (2, 4)))
    block_group = draw_block_group(jax.random.fold_in(key_of[16], 71), 0)
    req_group = with_ends(jax.random.randint(key_of[7], (REQS,), 0, 2), jax.random.fold_in(key_of[7], 1), 0, 1).astype(jnp.int32)
    lengths = ragged_sizes(key_of[8], REQS, REQS * TOK_DEV * 5 // 8, TOK_DEV, 0).astype(jnp.int32)
    w_out = gaussian(key_of[9], (HEADS * HD, D), (HEADS * HD) ** -0.5, 0.125, ((0, 4),))
    norm_gain = jnp.clip(1.0 + 0.15 * jax.random.normal(key_of[10], (D,), jnp.float32), 0.25, 1.75).astype(jnp.bfloat16)
    w_router = draw_w_router(jax.random.fold_in(key_of[16], 71), 0)
    routes_keys = jax.random.split(jax.random.fold_in(key_of[12], 1), TOKENS // TOK_DEV)
    routes_turns = jax.random.permutation(jax.random.fold_in(key_of[12], 3), TOKENS // TOK_DEV)
    routes = jax.vmap(lambda own, number: shared_out(jax.random.fold_in(key_of[12], 2), own, number, TOK_DEV, E, TOPK, CAP, 0))(routes_keys, routes_turns).reshape((TOKENS, TOPK))
    w_gate = gaussian(key_of[13], (2 * E, D, FF // 2), D ** -0.5, 0.125, ((0, 8), (2, 4)))
    w_up = gaussian(key_of[14], (2 * E, D, FF // 2), D ** -0.5, 0.125, ((0, 8), (2, 4)))
    w_down = gaussian(key_of[15], (2 * E, FF // 2, D), FF ** -0.5, 0.1875, ((0, 8), (1, 4)))
    return {"hidden_in": hidden_in, "queries": queries, "keys_new": keys_new, "values_new": values_new, "prefix_keys": prefix_keys, "prefix_values": prefix_values, "block_group": block_group, "req_group": req_group, "lengths": lengths, "w_out": w_out, "norm_gain": norm_gain, "w_router": w_router, "routes": routes, "w_gate": w_gate, "w_up": w_up, "w_down": w_down}


epsilon = 1e-06

def slot_numbers(block_routes):
    flatten = block_routes.reshape(-1)
    chosen = (flatten[:, None] == jnp.arange(E, dtype=jnp.int32)[None, :]).astype(jnp.int32)
    earlier = jnp.cumsum(chosen, axis=0) - chosen
    return (flatten, lax.optimization_barrier(jnp.sum(earlier * chosen, axis=1)).astype(jnp.int32))

def reference(hidden_in, queries, keys_new, values_new, prefix_keys, prefix_values, block_group, req_group, lengths, w_out, norm_gain, w_router, routes, w_gate, w_up, w_down):
    factor = 1.0 / math.sqrt(HD)
    prefix_k = prefix_keys.reshape(PBLOCKS * BLK, HEADS, HD).astype(jnp.float32)
    prefix_v = prefix_values.reshape(PBLOCKS * BLK, HEADS, HD).astype(jnp.float32)
    key_group = jnp.repeat(block_group, BLK)

    def attend(operands):
        query_rows, key_rows, value_rows, group_id, length_now = operands
        all_keys = jnp.concatenate([prefix_k, key_rows.astype(jnp.float32)], axis=0)
        all_values = jnp.concatenate([prefix_v, value_rows.astype(jnp.float32)], axis=0)
        usable = jnp.concatenate([key_group == group_id, jnp.arange(TOK_DEV, dtype=jnp.int32) < length_now])
        scores = jnp.einsum('qhd,khd->hqk', query_rows.astype(jnp.float32), all_keys) * factor
        scores = jnp.where(usable[None, None, :], scores, -jnp.inf)
        top_score = lax.optimization_barrier(jnp.max(scores, axis=-1, keepdims=True))
        weights = jnp.exp(scores - top_score)
        totals = lax.optimization_barrier(jnp.sum(weights, axis=-1))
        rounded = lax.optimization_barrier(weights.astype(jnp.bfloat16)).astype(jnp.float32)
        mixed = jnp.einsum('hqk,khd->hqd', rounded, all_values) / totals[..., None]
        return jnp.transpose(mixed, (1, 0, 2)).reshape(TOK_DEV, HEADS * HD).astype(jnp.bfloat16)
    heads_out = lax.map(attend, (queries.reshape(REQS, TOK_DEV, HEADS, HD), keys_new.reshape(REQS, TOK_DEV, HEADS, HD), values_new.reshape(REQS, TOK_DEV, HEADS, HD), req_group, lengths))
    heads_out = heads_out.reshape(TOKENS, HEADS * HD)
    resid = hidden_in.astype(jnp.float32) + jnp.dot(heads_out, w_out, preferred_element_type=jnp.float32)
    mean_square = lax.optimization_barrier(jnp.mean(resid * resid, axis=-1, keepdims=True))
    normed = (resid * lax.rsqrt(mean_square + epsilon) * norm_gain.astype(jnp.float32)).astype(jnp.bfloat16)
    logits = jnp.dot(normed.astype(jnp.float32), w_router, precision=lax.Precision.HIGHEST)
    routed = jnp.take_along_axis(logits, routes, axis=1)
    gates = jax.nn.softmax(routed, axis=-1)

    def table_of(block_routes, block_gates, base):
        flatten, slot = slot_numbers(block_routes)
        rows = (base + jnp.arange(TOK_DEV * TOPK, dtype=jnp.int32) // TOPK).astype(jnp.int32)
        index_table = jnp.full((E, CAP), TOKENS, jnp.int32).at[flatten, slot].set(rows)
        gate_table = jnp.zeros((E, CAP), jnp.float32).at[flatten, slot].set(block_gates.reshape(-1))
        return (index_table, gate_table)
    bases = (jnp.arange(REQS, dtype=jnp.int32) * TOK_DEV).astype(jnp.int32)
    index_all, gate_all = jax.vmap(table_of)(routes.reshape(REQS, TOK_DEV, TOPK), gates.reshape(REQS, TOK_DEV, TOPK), bases)
    index_all = jnp.transpose(index_all, (1, 0, 2)).reshape(E, REQS * CAP)
    gate_all = jnp.transpose(gate_all, (1, 0, 2)).reshape(E, REQS * CAP)
    padded = jnp.concatenate([normed, jnp.zeros((1, D), jnp.bfloat16)], axis=0)
    part_size = FF // (2 * N_TP)

    def expert_step(total, operands):
        gate_w, up_w, down_w, index_row, gate_row = operands
        rows = padded[index_row]
        output = jnp.zeros((REQS * CAP, D), jnp.float32)
        for half_id in range(2):
            gate_val = jnp.dot(rows, gate_w[half_id], preferred_element_type=jnp.float32).reshape(-1, N_TP, part_size)
            up_val = jnp.dot(rows, up_w[half_id], preferred_element_type=jnp.float32).reshape(-1, N_TP, part_size)
            inner = (jax.nn.silu(gate_val) * up_val).astype(jnp.bfloat16)
            pieces = jnp.einsum('rtp,tpd->rtd', inner.astype(jnp.float32), down_w[half_id].reshape(N_TP, part_size, D).astype(jnp.float32))
            rounded = lax.optimization_barrier(pieces.astype(jnp.bfloat16)).astype(jnp.float32)
            output = output + lax.optimization_barrier(jnp.sum(rounded, axis=1))
        total = total.at[index_row].add(gate_row[:, None] * output, mode='drop')
        return (total, None)
    moe_out, _ = lax.scan(expert_step, jnp.zeros((TOKENS, D), jnp.float32), (w_gate.reshape(E, 2, D, FF // 2), w_up.reshape(E, 2, D, FF // 2), w_down.reshape(E, 2, FF // 2, D), index_all, gate_all))
    return (resid + moe_out).astype(jnp.bfloat16)
```

```python
import functools
import math

import jax
import jax.numpy as jnp
from jax import lax
from jax.experimental import pallas as pl
from jax.experimental.pallas import tpu as pltpu
from jax.sharding import PartitionSpec as P

HD = 128
E = 64
TOPK = 8
CAP = 10


epsilon = 1e-06


def slot_numbers(block_routes):
    flatten = block_routes.reshape(-1)
    chosen = (flatten[:, None] == jnp.arange(E, dtype=jnp.int32)[None, :]).astype(jnp.int32)
    earlier = jnp.cumsum(chosen, axis=0) - chosen
    return (flatten, jnp.sum(earlier * chosen, axis=1))


def wide_body(
    hidden_in,
    queries,
    keys_new,
    values_new,
    prefix_keys,
    prefix_values,
    block_group,
    req_group,
    lengths,
    w_out,
    norm_gain,
    w_router,
    routes,
    w_gate,
    w_up,
    w_down,
):
    row_count = queries.shape[0]
    local_heads = queries.shape[1] // HD
    width = hidden_in.shape[1]
    factor = 1.0 / math.sqrt(HD)
    query_rows = queries.reshape(row_count, local_heads, HD)
    key_rows = keys_new.reshape(row_count, local_heads, HD)
    value_rows = values_new.reshape(row_count, local_heads, HD)
    group_id = req_group[0].astype(jnp.float32)
    own_valid = jnp.arange(row_count) < lengths[0]
    scores = (
        jnp.einsum("qhd,khd->hqk", query_rows, key_rows, preferred_element_type=jnp.float32)
        * factor
    )
    scores = jnp.where(own_valid[None, None, :], scores, -jnp.inf)
    top_score = jnp.max(scores, axis=-1)
    weights = jnp.exp(scores - top_score[..., None])
    best = top_score
    total = jnp.sum(weights, axis=-1)
    summed = jnp.einsum(
        "hqk,khd->hqd", weights.astype(jnp.bfloat16), value_rows, preferred_element_type=jnp.float32
    )
    piece_keys = lax.all_gather(prefix_keys, "req", axis=0, tiled=True)
    piece_values = lax.all_gather(prefix_values, "req", axis=0, tiled=True)
    piece_groups = lax.all_gather(block_group.astype(jnp.bfloat16), "req", axis=0, tiled=True)
    count = piece_keys.shape[0] * piece_keys.shape[1]
    flat_keys = piece_keys.reshape(count, local_heads, HD)
    flat_values = piece_values.reshape(count, local_heads, HD)
    key_valid = jnp.repeat(piece_groups.astype(jnp.float32), piece_keys.shape[1]) == group_id
    block_scores = (
        jnp.einsum("qhd,khd->hqk", query_rows, flat_keys, preferred_element_type=jnp.float32)
        * factor
    )
    block_scores = jnp.where(key_valid[None, None, :], block_scores, -jnp.inf)
    new_best = jnp.maximum(best, jnp.max(block_scores, axis=-1))
    shrink = jnp.exp(best - new_best)
    block_weights = jnp.exp(block_scores - new_best[..., None])
    added = jnp.einsum(
        "hqk,khd->hqd",
        block_weights.astype(jnp.bfloat16),
        flat_values,
        preferred_element_type=jnp.float32,
    )
    best, total, summed = (
        new_best,
        total * shrink + jnp.sum(block_weights, axis=-1),
        summed * shrink[..., None] + added,
    )
    mixed = (summed / total[..., None]).astype(jnp.bfloat16)
    mixed = jnp.transpose(mixed, (1, 0, 2)).reshape(row_count, local_heads * HD)
    partial_value = jnp.dot(mixed, w_out, preferred_element_type=jnp.float32)
    tp_count = lax.axis_size("tp")
    col_width = width // tp_count
    col_start = lax.axis_index("tp") * col_width
    whole = hidden_in.astype(jnp.float32) + lax.psum(
        partial_value.astype(jnp.bfloat16), "tp"
    ).astype(jnp.float32)
    mean_square = jnp.mean(whole * whole, axis=1, keepdims=True)
    normed = (
        whole * lax.rsqrt(mean_square + epsilon) * norm_gain.astype(jnp.float32)[None, :]
    ).astype(jnp.bfloat16)
    state_cols = lax.dynamic_slice_in_dim(whole, col_start, col_width, 1)
    logits = jnp.dot(normed.astype(jnp.float32), w_router, precision=lax.Precision.HIGHEST)
    expert_ids = jnp.arange(E, dtype=jnp.int32)
    picked = jnp.sum(
        jnp.where(routes[:, :, None] == expert_ids[None, None, :], logits[:, None, :], 0.0), axis=2
    )
    gates = jax.nn.softmax(picked, axis=1)
    flatten, slot = slot_numbers(routes)
    position = (flatten * CAP + slot).reshape(row_count, TOPK)
    columns = jnp.arange(E * CAP, dtype=jnp.int32)
    hits = position[:, :, None] == columns[None, None, :]
    placing = jnp.any(hits, axis=1).astype(jnp.bfloat16)
    outgoing = jnp.einsum("tc,td->cd", placing, normed, preferred_element_type=jnp.float32).astype(
        jnp.bfloat16
    )
    combining = jnp.sum(jnp.where(hits, gates[:, :, None], 0.0), axis=1)
    doubled = jnp.repeat(outgoing.reshape(E, CAP, width), 2, axis=0)
    received = lax.all_to_all(doubled, "req", split_axis=0, concat_axis=1, tiled=True)
    gate_val = jnp.einsum("lrd,ldf->lrf", received, w_gate, preferred_element_type=jnp.float32)
    up_val = jnp.einsum("lrd,ldf->lrf", received, w_up, preferred_element_type=jnp.float32)
    inner = (jax.nn.silu(gate_val) * up_val).astype(jnp.bfloat16)
    pieces = jnp.einsum("lrf,lfd->lrd", inner, w_down, preferred_element_type=jnp.float32).astype(
        jnp.bfloat16
    )
    returned = lax.all_to_all(pieces, "req", split_axis=1, concat_axis=0, tiled=True)
    summed_halves = jnp.sum(returned.reshape(E, 2, CAP, width).astype(jnp.float32), axis=1).reshape(
        E * CAP, width
    )
    expert_part = jnp.dot(
        combining,
        summed_halves,
        precision=lax.Precision.HIGHEST,
        preferred_element_type=jnp.float32,
    )
    expert_cols = lax.psum_scatter(
        expert_part.astype(jnp.bfloat16), "tp", scatter_dimension=1, tiled=True
    ).astype(jnp.float32)
    return (state_cols + expert_cols).astype(jnp.bfloat16)


EXT = 128
MESH = pl.DeviceIdType.MESH


def layer_kernel(
    n_req,
    n_tp,
    req_group,
    lengths,
    hidden,
    gain,
    queries,
    keys,
    values,
    prefix,
    routes,
    router,
    w_out_hbm,
    w_gate_hbm,
    w_up_hbm,
    w_down_hbm,
    out,
    w_out,
    w_gate,
    w_up,
    w_down,
    pre,
    heads,
    proj,
    proj_in,
    resid,
    rows_all,
    gates,
    scale,
    inner,
    part,
    core_in,
    core_sum,
    x_in,
    x_sum,
    y_in,
    y_sum,
    z_in,
    load_sem,
    pre_send,
    pre_recv,
    proj_send,
    proj_recv,
    gz_send,
    gz_recv,
    gy_send,
    gy_recv,
    gx_send,
    gx_recv,
    gc_send,
    gc_recv,
    rc_send,
    rc_recv,
    rx_send,
    rx_recv,
    ry_send,
    ry_recv,
    rz_send,
    rz_recv,
):
    rows, cols = hidden.shape
    n_z = n_req // 2
    total = n_req * rows
    req, tp = lax.axis_index("req"), lax.axis_index("tp")
    z, y = req // 2, req % 2
    x, core = tp // 2, tp % 2
    y_peer = z * 2 + (1 - y)
    x_peer = (1 - x) * 2 + core
    c_peer = x * 2 + (1 - core)

    loads = [
        pltpu.make_async_copy(source, target, load_sem.at[i])
        for i, (source, target) in enumerate(
            [(w_out_hbm, w_out), (w_gate_hbm, w_gate), (w_up_hbm, w_up), (w_down_hbm, w_down)]
        )
    ]
    for load in loads:
        load.start()

    barrier = pltpu.get_barrier_semaphore()
    for k in range(1, n_req):
        pl.semaphore_signal(
            barrier, inc=1, device_id={"req": (req + k) % n_req}, device_id_type=MESH
        )
    for k in range(1, n_tp):
        pl.semaphore_signal(barrier, inc=1, device_id={"tp": (tp + k) % n_tp}, device_id_type=MESH)
    pl.semaphore_wait(barrier, n_req + n_tp - 2)

    def send(source, target, send_sem, recv_sem, axis, peer):
        copy = pltpu.make_async_remote_copy(
            src_ref=source,
            dst_ref=target,
            send_sem=send_sem,
            recv_sem=recv_sem,
            device_id={axis: peer},
            device_id_type=MESH,
        )
        copy.start()
        return copy

    copies = [
        send(prefix, pre.at[k], pre_send.at[k], pre_recv.at[k], "req", (req + k) % n_req)
        for k in range(1, n_req)
    ]
    pre[0] = prefix[...]
    for copy in copies:
        copy.wait()

    blk = prefix.shape[0] // 2
    n_pre = n_req * blk
    ones = jnp.full((rows, EXT), 1.0 / EXT, jnp.bfloat16)
    nt = (((1,), (1,)), ((), ()))
    groups = pre[:, :blk, cols:].reshape(n_pre, EXT)
    group_row = lax.dot_general(ones, groups, nt, preferred_element_type=jnp.float32)
    pre_seen = group_row == req_group[0].astype(jnp.float32)
    own_seen = lax.broadcasted_iota(jnp.int32, (rows, rows), 1) < lengths[0]
    factor = 1.0 / math.sqrt(HD)
    for h in range(cols // HD):
        lanes = slice(h * HD, (h + 1) * HD)
        q = queries[:, lanes]
        pre_k = pre[:, :blk, lanes].reshape(n_pre, HD)
        pre_v = pre[:, blk:, lanes].reshape(n_pre, HD)
        s_pre = lax.dot_general(q, pre_k, nt, preferred_element_type=jnp.float32) * factor
        s_own = (
            lax.dot_general(q, keys[:, lanes], nt, preferred_element_type=jnp.float32) * factor
        )
        s_pre = jnp.where(pre_seen, s_pre, -jnp.inf)
        s_own = jnp.where(own_seen, s_own, -jnp.inf)
        top = jnp.maximum(
            jnp.max(s_pre, axis=1, keepdims=True), jnp.max(s_own, axis=1, keepdims=True)
        )
        p_pre, p_own = jnp.exp(s_pre - top), jnp.exp(s_own - top)
        denom = jnp.sum(p_pre, axis=1, keepdims=True) + jnp.sum(p_own, axis=1, keepdims=True)
        mixed = jnp.dot(p_pre.astype(jnp.bfloat16), pre_v, preferred_element_type=jnp.float32)
        mixed = mixed + jnp.dot(
            p_own.astype(jnp.bfloat16), values[:, lanes], preferred_element_type=jnp.float32
        )
        heads[:, lanes] = (mixed / denom).astype(jnp.bfloat16)

    loads[0].wait()
    for t in range(n_tp):
        proj[t] = jnp.dot(
            heads[...], w_out[:, t * cols : (t + 1) * cols], preferred_element_type=jnp.float32
        ).astype(jnp.bfloat16)
    copies = []
    for k in range(1, n_tp):
        peer = (tp + k) % n_tp
        copies.append(
            send(proj.at[peer], proj_in.at[k], proj_send.at[k], proj_recv.at[k], "tp", peer)
        )
    chunk = hidden[...].astype(jnp.float32) + proj[tp].astype(jnp.float32)
    for copy in copies:
        copy.wait()
    for k in range(1, n_tp):
        chunk = chunk + proj_in[k].astype(jnp.float32)
    resid[...] = chunk

    lane = lax.broadcasted_iota(jnp.int32, (rows, EXT), 1)
    square = jnp.sum(chunk * chunk, axis=1, keepdims=True)
    high = square.astype(jnp.bfloat16).astype(jnp.float32)
    middle = (square - high).astype(jnp.bfloat16).astype(jnp.float32)
    low = square - high - middle
    extra = jnp.where(lane == 0, high, jnp.where(lane == 1, middle, 0.0))
    extra = jnp.where(lane == 2, low, extra)
    for k in range(TOPK):
        extra = jnp.where(lane == routes[:, k : k + 1] + (EXT - E), 1.0, extra)
    rows_all[tp, 0, 0, :, :cols] = (chunk * gain[...].astype(jnp.float32)).astype(jnp.bfloat16)
    rows_all[tp, 0, 0, :, cols:] = extra.astype(jnp.bfloat16)

    own = rows_all.at[tp, 0, 0]
    z_copies = [
        send(
            own,
            rows_all.at[tp, 0, k],
            gz_send.at[k],
            gz_recv.at[k],
            "req",
            ((z + k) % n_z) * 2 + y,
        )
        for k in range(1, n_z)
    ]
    for copy in z_copies:
        copy.wait()
    near = rows_all.at[tp, 0]
    far = rows_all.at[tp, 1]
    y_copy = send(near, far, gy_send, gy_recv, "req", y_peer)
    x_near = send(near, near, gx_send.at[0], gx_recv.at[0], "tp", x_peer)
    c_near = send(near, near, gc_send.at[0], gc_recv.at[0], "tp", c_peer)
    y_copy.wait()
    x_far = send(far, far, gx_send.at[1], gx_recv.at[1], "tp", x_peer)
    c_far = send(far, far, gc_send.at[1], gc_recv.at[1], "tp", c_peer)
    x_near.wait()
    over_near = rows_all.at[x_peer, 0]
    d_near = send(over_near, over_near, gc_send.at[2], gc_recv.at[2], "tp", c_peer)
    x_far.wait()
    over_far = rows_all.at[x_peer, 1]
    d_far = send(over_far, over_far, gc_send.at[3], gc_recv.at[3], "tp", c_peer)
    c_near.wait()
    c_far.wait()
    d_near.wait()
    d_far.wait()

    lane_all = lax.broadcasted_iota(jnp.int32, (total, EXT), 1)
    extras = jnp.zeros((total, EXT), jnp.float32)
    logits = jnp.zeros((total, 3 * EXT), jnp.float32)
    for t in range(n_tp):
        extras = extras + rows_all[t, :, :, :, cols:].reshape(total, EXT).astype(jnp.float32)
        logits = logits + jnp.dot(
            rows_all[t, :, :, :, :cols].reshape(total, cols),
            router[t * cols : (t + 1) * cols, :],
            preferred_element_type=jnp.float32,
        )
    squares = jnp.sum(jnp.where(lane_all < 3, extras, 0.0), axis=1, keepdims=True)
    factor_all = lax.rsqrt(squares / (n_tp * cols) + epsilon)
    routed = (lane_all >= EXT - E) & (extras > 0.5)
    logits = (logits[:, :EXT] + logits[:, EXT : 2 * EXT] + logits[:, 2 * EXT :]) * factor_all
    logits = jnp.where(routed, logits, -jnp.inf)
    powers = jnp.exp(logits - jnp.max(logits, axis=1, keepdims=True))
    gates[...] = powers / jnp.sum(powers, axis=1, keepdims=True)
    scale[...] = jnp.broadcast_to(factor_all, (total, EXT))

    halves, depth, units = w_gate.shape
    loads[1].wait()
    loads[2].wait()

    def half_step(j, carry):
        both = jnp.zeros((total, 2 * units), jnp.float32)
        for t in range(n_tp):
            weights = jnp.concatenate(
                [w_gate[j, t * cols : (t + 1) * cols, :], w_up[j, t * cols : (t + 1) * cols, :]],
                axis=1,
            )
            both = both + jnp.dot(
                rows_all[t, :, :, :, :cols].reshape(total, cols),
                weights,
                preferred_element_type=jnp.float32,
            )
        expert = (req * halves + j) // 2 + (EXT - E)
        gate_col = jnp.sum(
            jnp.where(lane_all == expert, gates[...], 0.0), axis=1, keepdims=True
        )
        gate_val = both[:, :units] * scale[:, :units]
        up_val = both[:, units:] * scale[:, :units]
        value = gate_val / (1.0 + jnp.exp(-gate_val)) * up_val * gate_col
        inner[:, pl.ds(pl.multiple_of(j * units, units), units)] = value.astype(jnp.bfloat16)
        return carry

    lax.fori_loop(0, halves, half_step, 0)
    loads[3].wait()

    def down(t):
        where = pl.ds(pl.multiple_of(t * cols, cols), cols)
        result = jnp.dot(
            inner[...],
            w_down[:, :, where].reshape(halves * units, cols),
            preferred_element_type=jnp.float32,
        )
        part[t] = result.astype(jnp.bfloat16).reshape(2, n_z, rows, cols)

    def plus(first, second):
        return (first.astype(jnp.float32) + second.astype(jnp.float32)).astype(jnp.bfloat16)

    down((1 - x) * 2 + (1 - core))
    over = send(
        part.at[(1 - x) * 2 + (1 - core)],
        core_in.at[0],
        rc_send.at[0],
        rc_recv.at[0],
        "tp",
        c_peer,
    )
    down((1 - x) * 2 + core)
    over.wait()
    x_copies = []
    for side in (1, 0):
        core_sum[0, side] = plus(part[(1 - x) * 2 + core, side], core_in[0, side])
        x_copies.append(
            send(
                core_sum.at[0, side],
                x_in.at[side],
                rx_send.at[side],
                rx_recv.at[side],
                "tp",
                x_peer,
            )
        )
    down(x * 2 + (1 - core))
    here = send(
        part.at[x * 2 + (1 - core)],
        core_in.at[1],
        rc_send.at[1],
        rc_recv.at[1],
        "tp",
        c_peer,
    )
    down(x * 2 + core)
    here.wait()
    x_copies[0].wait()
    x_sum[1] = (
        part[x * 2 + core, 1].astype(jnp.float32)
        + core_in[1, 1].astype(jnp.float32)
        + x_in[1].astype(jnp.float32)
    ).astype(jnp.bfloat16)
    y_copy = send(x_sum.at[1], y_in, ry_send, ry_recv, "req", y_peer)
    x_copies[1].wait()
    near_sum = (
        part[x * 2 + core, 0].astype(jnp.float32)
        + core_in[1, 0].astype(jnp.float32)
        + x_in[0].astype(jnp.float32)
    )
    y_copy.wait()
    near_sum = near_sum + y_in[...].astype(jnp.float32)
    y_sum[...] = near_sum.astype(jnp.bfloat16)
    z_copies = [
        send(
            y_sum.at[k],
            z_in.at[k],
            rz_send.at[k],
            rz_recv.at[k],
            "req",
            ((z + n_z - k) % n_z) * 2 + y,
        )
        for k in range(1, n_z)
    ]
    result = resid[...] + near_sum[0]
    for copy in z_copies:
        copy.wait()
    for k in range(1, n_z):
        result = result + z_in[k].astype(jnp.float32)
    out[...] = result.astype(jnp.bfloat16)


def split_router(w_router):
    rest, pieces = w_router, []
    for _ in range(3):
        piece = lax.reduce_precision(rest, 8, 7)
        pieces.append(jnp.pad(piece, ((0, 0), (EXT - E, 0))).astype(jnp.bfloat16))
        rest = rest - piece
    return jnp.concatenate(pieces, axis=1)


def body(
    hidden_in,
    queries,
    keys_new,
    values_new,
    prefix_keys,
    prefix_values,
    block_group,
    req_group,
    lengths,
    w_out,
    norm_gain,
    w_router,
    routes,
    w_gate,
    w_up,
    w_down,
):
    n_req, n_tp = lax.axis_size("req"), lax.axis_size("tp")
    rows, width = hidden_in.shape
    cols = width // n_tp
    blk = prefix_keys.shape[1]
    start = lax.axis_index("tp") * cols
    hidden = lax.dynamic_slice_in_dim(hidden_in, start, cols, 1)
    gain = lax.dynamic_slice_in_dim(norm_gain, start, cols, 0).reshape(1, cols)
    both = jnp.concatenate([prefix_keys[0], prefix_values[0]], axis=0)
    group = jnp.broadcast_to(block_group.astype(jnp.bfloat16)[:, None], (2 * blk, EXT))
    prefix = jnp.concatenate([both, group], axis=1)
    n_z = n_req // 2
    total = n_req * rows
    halves, _, units = w_gate.shape
    bf16, f32 = jnp.bfloat16, jnp.float32
    dma = pltpu.SemaphoreType.DMA
    vmem = pl.BlockSpec(memory_space=pltpu.VMEM)
    smem = pl.BlockSpec(memory_space=pltpu.SMEM)
    hbm = pl.BlockSpec(memory_space=pl.ANY)
    return pl.pallas_call(
        functools.partial(layer_kernel, n_req, n_tp),
        out_shape=jax.ShapeDtypeStruct((rows, cols), bf16),
        in_specs=[smem] * 2 + [vmem] * 8 + [hbm] * 4,
        out_specs=vmem,
        scratch_shapes=[
            pltpu.VMEM(w_out.shape, bf16),
            pltpu.VMEM(w_gate.shape, bf16),
            pltpu.VMEM(w_up.shape, bf16),
            pltpu.VMEM(w_down.shape, bf16),
            pltpu.VMEM((n_req, 2 * blk, cols + EXT), bf16),
            pltpu.VMEM((rows, cols), bf16),
            pltpu.VMEM((n_tp, rows, cols), bf16),
            pltpu.VMEM((n_tp, rows, cols), bf16),
            pltpu.VMEM((rows, cols), f32),
            pltpu.VMEM((n_tp, 2, n_z, rows, cols + EXT), bf16),
            pltpu.VMEM((total, EXT), f32),
            pltpu.VMEM((total, EXT), f32),
            pltpu.VMEM((total, halves * units), bf16),
            pltpu.VMEM((n_tp, 2, n_z, rows, cols), bf16),
            pltpu.VMEM((2, 2, n_z, rows, cols), bf16),
            pltpu.VMEM((1, 2, n_z, rows, cols), bf16),
            pltpu.VMEM((2, n_z, rows, cols), bf16),
            pltpu.VMEM((2, n_z, rows, cols), bf16),
            pltpu.VMEM((n_z, rows, cols), bf16),
            pltpu.VMEM((n_z, rows, cols), bf16),
            pltpu.VMEM((n_z, rows, cols), bf16),
            dma((4,)),
            dma((n_req,)),
            dma((n_req,)),
            dma((n_tp,)),
            dma((n_tp,)),
            dma((n_z,)),
            dma((n_z,)),
            dma,
            dma,
            dma((2,)),
            dma((2,)),
            dma((4,)),
            dma((4,)),
            dma((2,)),
            dma((2,)),
            dma((2,)),
            dma((2,)),
            dma,
            dma,
            dma((n_z,)),
            dma((n_z,)),
        ],
        compiler_params=pltpu.CompilerParams(
            collective_id=0, has_side_effects=True, vmem_limit_bytes=56 * 1024 * 1024
        ),
    )(
        req_group,
        lengths,
        hidden,
        gain,
        queries,
        keys_new,
        values_new,
        prefix,
        routes,
        split_router(w_router),
        w_out,
        w_gate,
        w_up,
        w_down,
    )


def solution(mesh):
    in_specs = (
        P("req", None),
        P("req", "tp"),
        P("req", "tp"),
        P("req", "tp"),
        P("req", None, "tp"),
        P("req", None, "tp"),
        P("req"),
        P("req"),
        P("req"),
        P("tp", None),
        P(),
        P(),
        P("req", None),
        P("req", None, "tp"),
        P("req", None, "tp"),
        P("req", "tp", None),
    )
    out_specs = P("req", "tp")
    n_req, n_tp = mesh.shape["req"], mesh.shape["tp"]
    fits = n_req <= 8 and n_req % 2 == 0 and n_tp == 4
    return jax.shard_map(body if fits else wide_body, mesh=mesh, in_specs=in_specs, out_specs=out_specs, check_vma=False)
```

```python
import functools
import math

import jax
import jax.numpy as jnp
from jax import lax
from jax.experimental import pallas as pl
from jax.experimental.pallas import tpu as pltpu
from jax.sharding import PartitionSpec as P

HD = 128
E = 64
TOPK = 8
CAP = 10


epsilon = 1e-06


def slot_numbers(block_routes):
    flatten = block_routes.reshape(-1)
    chosen = (flatten[:, None] == jnp.arange(E, dtype=jnp.int32)[None, :]).astype(jnp.int32)
    earlier = jnp.cumsum(chosen, axis=0) - chosen
    return (flatten, jnp.sum(earlier * chosen, axis=1))


def wide_body(
    hidden_in,
    queries,
    keys_new,
    values_new,
    prefix_keys,
    prefix_values,
    block_group,
    req_group,
    lengths,
    w_out,
    norm_gain,
    w_router,
    routes,
    w_gate,
    w_up,
    w_down,
):
    row_count = queries.shape[0]
    local_heads = queries.shape[1] // HD
    width = hidden_in.shape[1]
    factor = 1.0 / math.sqrt(HD)
    query_rows = queries.reshape(row_count, local_heads, HD)
    key_rows = keys_new.reshape(row_count, local_heads, HD)
    value_rows = values_new.reshape(row_count, local_heads, HD)
    group_id = req_group[0].astype(jnp.float32)
    own_valid = jnp.arange(row_count) < lengths[0]
    scores = (
        jnp.einsum("qhd,khd->hqk", query_rows, key_rows, preferred_element_type=jnp.float32)
        * factor
    )
    scores = jnp.where(own_valid[None, None, :], scores, -jnp.inf)
    top_score = jnp.max(scores, axis=-1)
    weights = jnp.exp(scores - top_score[..., None])
    best = top_score
    total = jnp.sum(weights, axis=-1)
    summed = jnp.einsum(
        "hqk,khd->hqd", weights.astype(jnp.bfloat16), value_rows, preferred_element_type=jnp.float32
    )
    piece_keys = lax.all_gather(prefix_keys, "req", axis=0, tiled=True)
    piece_values = lax.all_gather(prefix_values, "req", axis=0, tiled=True)
    piece_groups = lax.all_gather(block_group.astype(jnp.bfloat16), "req", axis=0, tiled=True)
    count = piece_keys.shape[0] * piece_keys.shape[1]
    flat_keys = piece_keys.reshape(count, local_heads, HD)
    flat_values = piece_values.reshape(count, local_heads, HD)
    key_valid = jnp.repeat(piece_groups.astype(jnp.float32), piece_keys.shape[1]) == group_id
    block_scores = (
        jnp.einsum("qhd,khd->hqk", query_rows, flat_keys, preferred_element_type=jnp.float32)
        * factor
    )
    block_scores = jnp.where(key_valid[None, None, :], block_scores, -jnp.inf)
    new_best = jnp.maximum(best, jnp.max(block_scores, axis=-1))
    shrink = jnp.exp(best - new_best)
    block_weights = jnp.exp(block_scores - new_best[..., None])
    added = jnp.einsum(
        "hqk,khd->hqd",
        block_weights.astype(jnp.bfloat16),
        flat_values,
        preferred_element_type=jnp.float32,
    )
    best, total, summed = (
        new_best,
        total * shrink + jnp.sum(block_weights, axis=-1),
        summed * shrink[..., None] + added,
    )
    mixed = (summed / total[..., None]).astype(jnp.bfloat16)
    mixed = jnp.transpose(mixed, (1, 0, 2)).reshape(row_count, local_heads * HD)
    partial_value = jnp.dot(mixed, w_out, preferred_element_type=jnp.float32)
    tp_count = lax.axis_size("tp")
    col_width = width // tp_count
    col_start = lax.axis_index("tp") * col_width
    whole = hidden_in.astype(jnp.float32) + lax.psum(
        partial_value.astype(jnp.bfloat16), "tp"
    ).astype(jnp.float32)
    mean_square = jnp.mean(whole * whole, axis=1, keepdims=True)
    normed = (
        whole * lax.rsqrt(mean_square + epsilon) * norm_gain.astype(jnp.float32)[None, :]
    ).astype(jnp.bfloat16)
    state_cols = lax.dynamic_slice_in_dim(whole, col_start, col_width, 1)
    logits = jnp.dot(normed.astype(jnp.float32), w_router, precision=lax.Precision.HIGHEST)
    expert_ids = jnp.arange(E, dtype=jnp.int32)
    picked = jnp.sum(
        jnp.where(routes[:, :, None] == expert_ids[None, None, :], logits[:, None, :], 0.0), axis=2
    )
    gates = jax.nn.softmax(picked, axis=1)
    flatten, slot = slot_numbers(routes)
    position = (flatten * CAP + slot).reshape(row_count, TOPK)
    columns = jnp.arange(E * CAP, dtype=jnp.int32)
    hits = position[:, :, None] == columns[None, None, :]
    placing = jnp.any(hits, axis=1).astype(jnp.bfloat16)
    outgoing = jnp.einsum("tc,td->cd", placing, normed, preferred_element_type=jnp.float32).astype(
        jnp.bfloat16
    )
    combining = jnp.sum(jnp.where(hits, gates[:, :, None], 0.0), axis=1)
    doubled = jnp.repeat(outgoing.reshape(E, CAP, width), 2, axis=0)
    received = lax.all_to_all(doubled, "req", split_axis=0, concat_axis=1, tiled=True)
    gate_val = jnp.einsum("lrd,ldf->lrf", received, w_gate, preferred_element_type=jnp.float32)
    up_val = jnp.einsum("lrd,ldf->lrf", received, w_up, preferred_element_type=jnp.float32)
    inner = (jax.nn.silu(gate_val) * up_val).astype(jnp.bfloat16)
    pieces = jnp.einsum("lrf,lfd->lrd", inner, w_down, preferred_element_type=jnp.float32).astype(
        jnp.bfloat16
    )
    returned = lax.all_to_all(pieces, "req", split_axis=1, concat_axis=0, tiled=True)
    summed_halves = jnp.sum(returned.reshape(E, 2, CAP, width).astype(jnp.float32), axis=1).reshape(
        E * CAP, width
    )
    expert_part = jnp.dot(
        combining,
        summed_halves,
        precision=lax.Precision.HIGHEST,
        preferred_element_type=jnp.float32,
    )
    expert_cols = lax.psum_scatter(
        expert_part.astype(jnp.bfloat16), "tp", scatter_dimension=1, tiled=True
    ).astype(jnp.float32)
    return (state_cols + expert_cols).astype(jnp.bfloat16)


EXT = 128
MESH = pl.DeviceIdType.MESH


def layer_kernel(
    n_req,
    n_tp,
    req_group,
    lengths,
    block_group,
    hidden,
    gain,
    queries,
    keys,
    values,
    prefix_keys,
    prefix_values,
    routes,
    w_router,
    w_out_hbm,
    w_gate_hbm,
    w_up_hbm,
    w_down_hbm,
    out,
    w_out,
    w_gate,
    w_up,
    w_down,
    router,
    pre,
    heads,
    proj,
    proj_in,
    resid,
    rows_all,
    gates,
    scale,
    inner,
    part,
    core_in,
    core_sum,
    x_in,
    x_sum,
    y_in,
    y_sum,
    z_in,
    load_sem,
    pre_send,
    pre_recv,
    proj_send,
    proj_recv,
    gz_send,
    gz_recv,
    gy_send,
    gy_recv,
    gx_send,
    gx_recv,
    gc_send,
    gc_recv,
    rc_send,
    rc_recv,
    rx_send,
    rx_recv,
    ry_send,
    ry_recv,
    rz_send,
    rz_recv,
):
    rows, cols = queries.shape
    blk = prefix_keys.shape[1]
    n_z = n_req // 2
    total = n_z * rows
    order = sorted(range(n_z), key=lambda k: min(k, n_z - k))
    req, tp = lax.axis_index("req"), lax.axis_index("tp")
    z, y = req // 2, req % 2
    x, core = tp // 2, tp % 2
    y_peer = z * 2 + (1 - y)
    x_peer = (1 - x) * 2 + core
    c_peer = x * 2 + (1 - core)

    loads = [
        pltpu.make_async_copy(source, target, load_sem.at[i])
        for i, (source, target) in enumerate(
            [(w_out_hbm, w_out), (w_gate_hbm, w_gate), (w_up_hbm, w_up), (w_down_hbm, w_down)]
        )
    ]
    for load in loads:
        load.start()

    pre[0, :blk, :cols] = prefix_keys[0]
    pre[0, blk:, :cols] = prefix_values[0]
    pre[0, :, cols:] = jnp.full((2 * blk, EXT), block_group[0].astype(jnp.float32)).astype(
        jnp.bfloat16
    )

    barrier = pltpu.get_barrier_semaphore()
    for k in range(1, n_req):
        pl.semaphore_signal(
            barrier, inc=1, device_id={"req": (req + k) % n_req}, device_id_type=MESH
        )
    for k in range(1, n_tp):
        pl.semaphore_signal(barrier, inc=1, device_id={"tp": (tp + k) % n_tp}, device_id_type=MESH)
    pl.semaphore_wait(barrier, n_req + n_tp - 2)

    def send(source, target, send_sem, recv_sem, axis, peer):
        copy = pltpu.make_async_remote_copy(
            src_ref=source,
            dst_ref=target,
            send_sem=send_sem,
            recv_sem=recv_sem,
            device_id={axis: peer},
            device_id_type=MESH,
        )
        copy.start()
        return copy

    copies = [
        send(pre.at[0], pre.at[k], pre_send.at[k], pre_recv.at[k], "req", (req + k) % n_req)
        for k in range(1, n_req)
    ]
    rest = w_router[...]
    for i in range(3):
        piece = rest.astype(jnp.bfloat16)
        router[i * EXT : i * EXT + EXT - E, :] = jnp.zeros_like(piece)
        router[i * EXT + EXT - E : (i + 1) * EXT, :] = piece
        rest = rest - piece.astype(jnp.float32)
    for copy in copies:
        copy.wait()

    n_pre = n_req * blk
    ones = jnp.full((rows, EXT), 1.0 / EXT, jnp.bfloat16)
    nt = (((1,), (1,)), ((), ()))
    groups = pre[:, :blk, cols:].reshape(n_pre, EXT)
    group_row = lax.dot_general(ones, groups, nt, preferred_element_type=jnp.float32)
    pre_seen = group_row == req_group[0].astype(jnp.float32)
    own_seen = lax.broadcasted_iota(jnp.int32, (rows, rows), 1) < lengths[0]
    factor = 1.0 / math.sqrt(HD)
    for h in range(cols // HD):
        lanes = slice(h * HD, (h + 1) * HD)
        q = queries[:, lanes]
        pre_k = pre[:, :blk, lanes].reshape(n_pre, HD)
        pre_v = pre[:, blk:, lanes].reshape(n_pre, HD)
        s_pre = lax.dot_general(q, pre_k, nt, preferred_element_type=jnp.float32) * factor
        s_own = (
            lax.dot_general(q, keys[:, lanes], nt, preferred_element_type=jnp.float32) * factor
        )
        s_pre = jnp.where(pre_seen, s_pre, -jnp.inf)
        s_own = jnp.where(own_seen, s_own, -jnp.inf)
        top = jnp.maximum(
            jnp.max(s_pre, axis=1, keepdims=True), jnp.max(s_own, axis=1, keepdims=True)
        )
        p_pre, p_own = jnp.exp(s_pre - top), jnp.exp(s_own - top)
        denom = jnp.sum(p_pre, axis=1, keepdims=True) + jnp.sum(p_own, axis=1, keepdims=True)
        mixed = jnp.dot(p_pre.astype(jnp.bfloat16), pre_v, preferred_element_type=jnp.float32)
        mixed = mixed + jnp.dot(
            p_own.astype(jnp.bfloat16), values[:, lanes], preferred_element_type=jnp.float32
        )
        heads[:, lanes] = (mixed / denom).astype(jnp.bfloat16)

    loads[0].wait()
    for t in range(n_tp):
        proj[t] = jnp.dot(
            heads[...], w_out[:, t * cols : (t + 1) * cols], preferred_element_type=jnp.float32
        ).astype(jnp.bfloat16)
    copies = []
    for k in range(1, n_tp):
        peer = (tp + k) % n_tp
        copies.append(
            send(proj.at[peer], proj_in.at[k], proj_send.at[k], proj_recv.at[k], "tp", peer)
        )
    own_cols = pl.ds(pl.multiple_of(tp * cols, cols), cols)
    chunk = hidden[:, own_cols].astype(jnp.float32) + proj[tp].astype(jnp.float32)
    for copy in copies:
        copy.wait()
    for k in range(1, n_tp):
        chunk = chunk + proj_in[k].astype(jnp.float32)
    resid[...] = chunk

    lane = lax.broadcasted_iota(jnp.int32, (rows, EXT), 1)
    square = jnp.sum(chunk * chunk, axis=1, keepdims=True)
    high = square.astype(jnp.bfloat16).astype(jnp.float32)
    middle = (square - high).astype(jnp.bfloat16).astype(jnp.float32)
    low = square - high - middle
    extra = jnp.where(lane == 0, high, jnp.where(lane == 1, middle, 0.0))
    extra = jnp.where(lane == 2, low, extra)
    experts = lax.broadcasted_iota(jnp.int32, (EXT, rows), 0) - (EXT - E)
    named = jnp.zeros((EXT, rows), jnp.float32)
    for k in range(TOPK):
        named = jnp.where(experts == routes[k : k + 1, :], 1.0, named)
    first = lax.broadcasted_iota(jnp.int32, (rows, rows), 0)
    second = lax.broadcasted_iota(jnp.int32, (rows, rows), 1)
    eye = jnp.where(first == second, 1.0, 0.0).astype(jnp.bfloat16)
    extra = extra + lax.dot_general(
        eye, named.astype(jnp.bfloat16), nt, preferred_element_type=jnp.float32
    )
    rows_all[tp, 0, 0, :, :cols] = (chunk * gain[:, own_cols].astype(jnp.float32)).astype(jnp.bfloat16)
    rows_all[tp, 0, 0, :, cols:] = extra.astype(jnp.bfloat16)

    own = rows_all.at[tp, 0, 0]
    z_copies = [
        send(
            own,
            rows_all.at[tp, 0, k],
            gz_send.at[k],
            gz_recv.at[k],
            "req",
            ((z + k) % n_z) * 2 + y,
        )
        for k in range(1, n_z)
    ]
    arrived = {k: copy for k, copy in zip(range(1, n_z), z_copies)}
    y_copies, x_near, c_near, x_far, c_far, d_near, d_far = {}, {}, {}, {}, {}, {}, {}

    def over_x(side, k):
        block = rows_all.at[tp, side, k]
        return send(block, block, gx_send.at[side, k], gx_recv.at[side, k], "tp", x_peer)

    def over_core(owner, i, side, k):
        block = rows_all.at[owner, side, k]
        return send(block, block, gc_send.at[i, side, k], gc_recv.at[i, side, k], "tp", c_peer)

    for k in order:
        if k > 0:
            arrived[k].wait()
        x_near[k] = over_x(0, k)
        y_copies[k] = send(
            rows_all.at[tp, 0, k],
            rows_all.at[tp, 1, k],
            gy_send.at[k],
            gy_recv.at[k],
            "req",
            y_peer,
        )
        c_near[k] = over_core(tp, 0, 0, k)
    for k in order:
        x_near[k].wait()
        d_near[k] = over_core(x_peer, 1, 0, k)
    for k in order:
        y_copies[k].wait()
        x_far[k] = over_x(1, k)
        c_far[k] = over_core(tp, 0, 1, k)
    for k in order:
        c_near[k].wait()
        d_near[k].wait()

    halves, depth, units = w_gate.shape
    lane_all = lax.broadcasted_iota(jnp.int32, (total, EXT), 1)

    def rows_of(side):
        return jnp.concatenate(
            [rows_all[t, side, :, :, :cols].reshape(total, cols) for t in range(n_tp)], axis=1
        )

    def find_gates(side):
        extras = jnp.zeros((total, EXT), jnp.float32)
        for t in range(n_tp):
            extras = extras + rows_all[t, side, :, :, cols:].reshape(total, EXT).astype(jnp.float32)
        logits = lax.dot_general(
            rows_of(side), router[...], nt, preferred_element_type=jnp.float32
        )
        squares = jnp.sum(jnp.where(lane_all < 3, extras, 0.0), axis=1, keepdims=True)
        factor_all = lax.rsqrt(squares / (n_tp * cols) + epsilon)
        routed = (lane_all >= EXT - E) & (extras > 0.5)
        logits = (logits[:, :EXT] + logits[:, EXT : 2 * EXT] + logits[:, 2 * EXT :]) * factor_all
        logits = jnp.where(routed, logits, -jnp.inf)
        powers = jnp.exp(logits - jnp.max(logits, axis=1, keepdims=True))
        gates[...] = powers / jnp.sum(powers, axis=1, keepdims=True)
        scale[...] = jnp.broadcast_to(factor_all, (total, EXT))

    def hidden_units(side, begin, end):
        def half_step(j, carry):
            weights = jnp.concatenate([w_gate[j], w_up[j]], axis=1)
            both = jnp.dot(rows_of(side), weights, preferred_element_type=jnp.float32)
            expert = (req * halves + j) // 2 + (EXT - E)
            gate_col = jnp.sum(
                jnp.where(lane_all == expert, gates[...], 0.0), axis=1, keepdims=True
            )
            gate_val = both[:, :units] * scale[:, :units]
            up_val = both[:, units:] * scale[:, :units]
            value = gate_val / (1.0 + jnp.exp(-gate_val)) * up_val * gate_col
            inner[:, pl.ds(pl.multiple_of(j * units, units), units)] = value.astype(jnp.bfloat16)
            return carry

        lax.fori_loop(begin, end, half_step, 0, unroll=2)

    def down(side, t):
        where = pl.ds(pl.multiple_of(t * cols, cols), cols)
        result = jnp.dot(
            inner[...],
            w_down[:, :, where].reshape(halves * units, cols),
            preferred_element_type=jnp.float32,
        )
        part[t, side] = result.astype(jnp.bfloat16).reshape(n_z, rows, cols)

    def to_core(i, side, t):
        return send(
            part.at[t, side],
            core_in.at[i, side],
            rc_send.at[i, side],
            rc_recv.at[i, side],
            "tp",
            c_peer,
        )

    def to_x(side, k):
        mine = part[x_peer, side, k].astype(jnp.float32)
        core_sum[side, k] = (mine + core_in[0, side, k].astype(jnp.float32)).astype(jnp.bfloat16)
        return send(
            core_sum.at[side, k],
            x_in.at[side, k],
            rx_send.at[side, k],
            rx_recv.at[side, k],
            "tp",
            x_peer,
        )

    def three(side, k):
        return (
            part[tp, side, k].astype(jnp.float32)
            + core_in[1, side, k].astype(jnp.float32)
            + x_in[side, k].astype(jnp.float32)
        )

    over_t, here_t = (1 - x) * 2 + (1 - core), c_peer
    last = halves - halves // 4
    early = halves // 4

    find_gates(0)
    loads[1].wait()
    loads[2].wait()
    hidden_units(0, 0, last)
    for k in order:
        x_far[k].wait()
        d_far[k] = over_core(x_peer, 1, 1, k)
    hidden_units(0, last, halves)
    loads[3].wait()
    down(0, over_t)
    over = to_core(0, 0, over_t)
    down(0, here_t)
    here = to_core(1, 0, here_t)
    down(0, x_peer)
    down(0, tp)

    for k in order:
        c_far[k].wait()
        d_far[k].wait()
    find_gates(1)
    hidden_units(1, 0, early)
    over.wait()
    here.wait()
    x_first = [to_x(0, k) for k in range(n_z)]
    hidden_units(1, early, halves)
    down(1, over_t)
    over = to_core(0, 1, over_t)
    down(1, x_peer)
    over.wait()
    back = order[::-1]
    x_second = {k: to_x(1, k) for k in back}
    down(1, here_t)
    here = to_core(1, 1, here_t)
    down(1, tp)
    here.wait()
    for copy in x_first:
        copy.wait()
    y_back, z_back = {}, {}
    for k in back:
        x_second[k].wait()
        x_sum[k] = three(1, k).astype(jnp.bfloat16)
        y_back[k] = send(x_sum.at[k], y_in.at[k], ry_send.at[k], ry_recv.at[k], "req", y_peer)
    for k in back:
        near_sum = three(0, k)
        y_back[k].wait()
        near_sum = near_sum + y_in[k].astype(jnp.float32)
        if k == 0:
            resid[...] = resid[...] + near_sum
        else:
            y_sum[k] = near_sum.astype(jnp.bfloat16)
            z_back[k] = send(
                y_sum.at[k],
                z_in.at[k],
                rz_send.at[k],
                rz_recv.at[k],
                "req",
                ((z + n_z - k) % n_z) * 2 + y,
            )
    result = resid[...]
    for k in range(1, n_z):
        z_back[k].wait()
        result = result + z_in[k].astype(jnp.float32)
    out[...] = result.astype(jnp.bfloat16)


def body(
    hidden_in,
    queries,
    keys_new,
    values_new,
    prefix_keys,
    prefix_values,
    block_group,
    req_group,
    lengths,
    w_out,
    norm_gain,
    w_router,
    routes,
    w_gate,
    w_up,
    w_down,
):
    n_req, n_tp = lax.axis_size("req"), lax.axis_size("tp")
    rows, width = hidden_in.shape
    cols = width // n_tp
    blk = prefix_keys.shape[1]
    n_z = n_req // 2
    total = n_z * rows
    halves, _, units = w_gate.shape
    bf16, f32 = jnp.bfloat16, jnp.float32
    dma = pltpu.SemaphoreType.DMA
    vmem = pl.BlockSpec(memory_space=pltpu.VMEM)
    smem = pl.BlockSpec(memory_space=pltpu.SMEM)
    hbm = pl.BlockSpec(memory_space=pl.ANY)
    return pl.pallas_call(
        functools.partial(layer_kernel, n_req, n_tp),
        out_shape=jax.ShapeDtypeStruct((rows, cols), bf16),
        in_specs=[smem] * 3 + [vmem] * 9 + [hbm] * 4,
        out_specs=vmem,
        scratch_shapes=[
            pltpu.VMEM(w_out.shape, bf16),
            pltpu.VMEM(w_gate.shape, bf16),
            pltpu.VMEM(w_up.shape, bf16),
            pltpu.VMEM(w_down.shape, bf16),
            pltpu.VMEM((3 * EXT, width), bf16),
            pltpu.VMEM((n_req, 2 * blk, cols + EXT), bf16),
            pltpu.VMEM((rows, cols), bf16),
            pltpu.VMEM((n_tp, rows, cols), bf16),
            pltpu.VMEM((n_tp, rows, cols), bf16),
            pltpu.VMEM((rows, cols), f32),
            pltpu.VMEM((n_tp, 2, n_z, rows, cols + EXT), bf16),
            pltpu.VMEM((total, EXT), f32),
            pltpu.VMEM((total, EXT), f32),
            pltpu.VMEM((total, halves * units), bf16),
            pltpu.VMEM((n_tp, 2, n_z, rows, cols), bf16),
            pltpu.VMEM((2, 2, n_z, rows, cols), bf16),
            pltpu.VMEM((2, n_z, rows, cols), bf16),
            pltpu.VMEM((2, n_z, rows, cols), bf16),
            pltpu.VMEM((n_z, rows, cols), bf16),
            pltpu.VMEM((n_z, rows, cols), bf16),
            pltpu.VMEM((n_z, rows, cols), bf16),
            pltpu.VMEM((n_z, rows, cols), bf16),
            dma((4,)),
            dma((n_req,)),
            dma((n_req,)),
            dma((n_tp,)),
            dma((n_tp,)),
            dma((n_z,)),
            dma((n_z,)),
            dma((n_z,)),
            dma((n_z,)),
            dma((2, n_z)),
            dma((2, n_z)),
            dma((2, 2, n_z)),
            dma((2, 2, n_z)),
            dma((2, 2)),
            dma((2, 2)),
            dma((2, n_z)),
            dma((2, n_z)),
            dma((n_z,)),
            dma((n_z,)),
            dma((n_z,)),
            dma((n_z,)),
        ],
        compiler_params=pltpu.CompilerParams(
            collective_id=0, has_side_effects=True, vmem_limit_bytes=56 * 1024 * 1024
        ),
    )(
        req_group,
        lengths,
        block_group,
        hidden_in,
        norm_gain.reshape(1, width),
        queries,
        keys_new,
        values_new,
        prefix_keys,
        prefix_values,
        routes.T,
        w_router.T,
        w_out,
        w_gate,
        w_up,
        w_down,
    )


def solution(mesh):
    in_specs = (
        P("req", None),
        P("req", "tp"),
        P("req", "tp"),
        P("req", "tp"),
        P("req", None, "tp"),
        P("req", None, "tp"),
        P("req"),
        P("req"),
        P("req"),
        P("tp", None),
        P(),
        P(),
        P("req", None),
        P("req", None, "tp"),
        P("req", None, "tp"),
        P("req", "tp", None),
    )
    out_specs = P("req", "tp")
    n_req, n_tp = mesh.shape["req"], mesh.shape["tp"]
    fits = n_req <= 8 and n_req % 2 == 0 and n_tp == 4
    return jax.shard_map(body if fits else wide_body, mesh=mesh, in_specs=in_specs, out_specs=out_specs, check_vma=False)
```
